256 devices in a mesh: blk: 128 (over z, y, x), aux: 2 (over core).
Axes of the slice: x: 4, y: 4, z: 8, core: 2. Of those that a mesh axis runs over, the one named last changes fastest.
Arguments:
- three_centre: bfloat16 [16384, 4, 4096], P('blk', 'aux'), may hold values from -6 to 6
- occupied_blocks: bfloat16 [1024, 64, 64], P('blk'), may hold values from -1.5 to 1.5
- virtual_blocks: bfloat16 [1024, 64, 64], P('blk'), may hold values from -1.5 to 1.5
- row_slot: int32 [16384], P('blk'), may hold values from 0 to 7
- col_slot: int32 [16384], P('blk'), may hold values from 0 to 7
- block_owner: int32 [16384, 1], P('blk'), may hold values from 0 to 127; in each aligned block of 128 rows (0 to 127, 128 to 255, ...) at most 2 rows name the same one
Outputs:
- polarizability: float32 [1024, 4, 4], P('blk', 'aux')
The draws below stay inside these ranges and needn't reach their ends.
Inputs may be any that keep to these rules, and one draw needn't show every extreme that they name: `block_owner`: among the 128 blocks stored on one index of blk, no owner is named more than 2 times, a bound that some block reaches.
All inputs are finite; a program needn't handle non-finite values.
Results may differ from the reference program's by a relative error of at most 0.0003.
Values may be sent and summed in bfloat16 or wider, within the bound.
A program may use at most 64 MiB of HBM per device.

```python
import math
import jax
import jax.numpy as jnp
import numpy as np
from jax import lax

BS = 64
GD = 8
NB_DEV = 128
CAP = 2
NG = 1024
NB_TOT = 16384
NAUX = 4
N_BLK = 128


def density_draw(key, salt_value):
    base_key = jax.random.fold_in(key, salt_value)
    basis_one, basis_two, spread_key = jax.random.split(base_key, 3)
    left_basis = jnp.linalg.qr(jax.random.normal(basis_one, (NG, BS, BS), jnp.float32))[0]
    right_basis = jnp.linalg.qr(jax.random.normal(basis_two, (NG, BS, BS), jnp.float32))[0]
    spread = jax.random.uniform(spread_key, (NG, BS), jnp.float32)
    low_part = (jnp.arange(BS, dtype=jnp.int32) < BS // 4)[None, :]
    eigen_values = jnp.where(low_part, 0.02 + 0.9 * spread, 0.6 + spread)
    singular = jnp.sqrt(eigen_values)
    scaled = left_basis * singular[:, None, :]
    return jnp.einsum('gij,gkj->gik', scaled, right_basis, precision=lax.Precision.HIGHEST)


def draw_occupied_blocks(key, part):
    return density_draw(key, 11).astype(jnp.bfloat16)


def draw_virtual_blocks(key, part):
    return density_draw(key, 23).astype(jnp.bfloat16)


def set_ends(result, key, least, high):
    spot = [jax.random.randint(jax.random.fold_in(key, axis), (), 0, length) for axis, length in enumerate(result.shape)]
    widest = result.shape.index(max(result.shape))
    neighbour = spot[:widest] + [(spot[widest] + 1) % result.shape[widest]] + spot[widest + 1:]
    return result.at[tuple(spot)].set(least).at[tuple(neighbour)].set(high)


def shard_levels(own_key, extent, cuts, smallest, largest):
    def one(dim, shards_of):
        draws = jax.random.uniform(jax.random.fold_in(jax.random.fold_in(own_key, 6), dim), (shards_of,), jnp.float32, smallest / len(cuts), largest / len(cuts))
        return jnp.repeat(jnp.exp(draws), extent[dim] // shards_of).reshape((-1,) + (1,) * (len(extent) - dim - 1))

    factor_of = one(*cuts[0])
    for cut in cuts[1:]:
        factor_of = factor_of * one(*cut)
    return factor_of


def shared_out(rng, own, number, rows, number_of, top, limit, skew):
    order = jax.random.permutation(rng, number_of)
    crowded, common = load_shares(number_of, rows * top, limit, skew, True), load_shares(number_of, rows * top, limit, skew, False)
    places = jnp.arange(number_of)

    def named(sizes, turn):
        used = int((sizes > 0).sum())
        fixed = max(1, used // 4)
        shifted = fixed + (places - fixed + turn * (used - fixed)) % max(1, number_of - fixed)
        return jnp.zeros((number_of,), jnp.int32).at[order[jnp.where(places < fixed, places, shifted)]].set(jnp.asarray(sizes, jnp.int32))

    sizes = jnp.where(number % 4 == 0, named(crowded, number // 4), named(common, number - number // 4 - 1))
    mixed = jax.random.permutation(jax.random.fold_in(own, 3), number_of)
    donor, sink = mixed[0:number_of // 2 * 2:2], mixed[1:number_of // 2 * 2:2]
    room = jnp.minimum(sizes[donor] - 1, limit - sizes[sink]) // 2
    room = jnp.where((donor == order[0]) | (sink == order[0]) | (sizes[sink] == 0), 0, jnp.maximum(room, 0))
    shifted = jax.random.randint(jax.random.fold_in(own, 4), (number_of // 2,), 0, 1 << 20) % (room + 1)
    sizes = sizes.at[donor].add(-shifted).at[sink].add(shifted)
    labels = jnp.searchsorted(jnp.cumsum(sizes), jnp.arange(rows * top), side="right").astype(jnp.int32)
    grid = labels.reshape(top, rows).T
    grid = grid[jax.random.permutation(jax.random.fold_in(own, 1), rows)]
    turn = jax.random.randint(jax.random.fold_in(own, 2), (rows, 1), 0, top)
    return jnp.take_along_axis(grid, (jnp.arange(top)[None, :] + turn) % top, axis=1)


def load_shares(number_of, total, most, lean, full):
    weights = [(1 << 20) // math.isqrt(grade ** lean) + 1 for grade in range(1, number_of + 1)]
    largest = most if full else min(most, max(-(-total // number_of), total * weights[0] // sum(weights)))
    least = 1 if total - largest >= number_of - 1 else 0
    holding, rest = [largest] + [least] * (number_of - 1), total - largest - least * (number_of - 1)
    while rest > 0:
        candidates = [i for i in range(1, number_of) if holding[i] < largest] or [i for i in range(1, number_of) if holding[i] < most]
        pool, left = sum([weights[i] for i in candidates]), rest
        for i in candidates:
            extra = min(most - holding[i], max(1, left * weights[i] // pool), rest)
            holding[i] = holding[i] + extra
            rest = rest - extra
    return np.array(holding)


def noise(stream_key, dims, width, limit, pieces=(), kind=jnp.bfloat16):
    factor_of = shard_levels(stream_key, dims, pieces, -0.22, 0.18) if pieces else 1.0
    values = jax.random.normal(stream_key, dims, jnp.float32) * width * factor_of
    return jnp.minimum(jnp.maximum(values, -limit), limit).astype(kind)


def setup_inputs(seed: int = 0) -> dict:
    seeds = jax.random.split(jax.random.key(seed), 7)
    three_centre = noise(seeds[0], (NB_TOT, NAUX, BS * BS), 1.0, 6.0, ((0, 128), (1, 2)))
    occupied_blocks = draw_occupied_blocks(jax.random.fold_in(seeds[6], 71), 0)
    virtual_blocks = draw_virtual_blocks(jax.random.fold_in(seeds[6], 71), 0)
    row_slot = set_ends(jax.random.randint(seeds[3], (NB_TOT,), 0, GD), jax.random.fold_in(seeds[3], 1), 0, GD - 1).astype(jnp.int32)
    col_slot = set_ends(jax.random.randint(seeds[4], (NB_TOT,), 0, GD), jax.random.fold_in(seeds[4], 1), 0, GD - 1).astype(jnp.int32)
    block_owner_keys = jax.random.split(jax.random.fold_in(seeds[5], 1), NB_TOT // NB_DEV)
    block_owner_turns = jax.random.permutation(jax.random.fold_in(seeds[5], 3), NB_TOT // NB_DEV)
    block_owner = jax.vmap(lambda own, number: shared_out(jax.random.fold_in(seeds[5], 2), own, number, NB_DEV, N_BLK, 1, CAP, 2))(block_owner_keys, block_owner_turns).reshape((NB_TOT, 1))
    return {"three_centre": three_centre, "occupied_blocks": occupied_blocks, "virtual_blocks": virtual_blocks, "row_slot": row_slot, "col_slot": col_slot, "block_owner": block_owner}


def reference(three_centre, occupied_blocks, virtual_blocks, row_slot, col_slot, block_owner):
    scale = 0.25 / (BS * BS)
    owners = block_owner[:, 0]

    def one_device(chi, index):
        start = (index * NB_DEV).astype(jnp.int32)
        blocks = lax.dynamic_slice_in_dim(three_centre, start, NB_DEV, 0).reshape(NB_DEV, NAUX, BS, BS)
        rows = (index * GD + lax.dynamic_slice_in_dim(row_slot, start, NB_DEV, 0)).astype(jnp.int32)
        cols = (lax.dynamic_slice_in_dim(owners, start, NB_DEV, 0) * GD + lax.dynamic_slice_in_dim(col_slot, start, NB_DEV, 0)).astype(jnp.int32)
        occupied = occupied_blocks[rows].astype(jnp.float32)
        virtual = virtual_blocks[cols].astype(jnp.float32)
        half = jnp.einsum('kpmn,kml->kpln', blocks.astype(jnp.float32), occupied, precision=lax.Precision.HIGHEST).astype(jnp.bfloat16)
        full = jnp.einsum('kpln,kns->kpls', half.astype(jnp.float32), virtual, precision=lax.Precision.HIGHEST).astype(jnp.bfloat16)
        flat = full.reshape(NB_DEV, NAUX, BS * BS).astype(jnp.float32)
        terms = jnp.einsum('kpc,kqc->kpq', flat, flat, precision=lax.Precision.HIGHEST) * scale
        chi = chi.at[cols].add(terms)
        return (chi, None)
    start_chi = jnp.zeros((NG, NAUX, NAUX), jnp.float32)
    chi, _ = lax.scan(one_device, start_chi, jnp.arange(N_BLK, dtype=jnp.int32))
    return chi
```

```python
import functools

import jax
import jax.numpy as jnp
from jax import lax
from jax.experimental import pallas as pl
from jax.experimental.pallas import tpu as pltpu
from jax.sharding import PartitionSpec as P

MESH = pl.DeviceIdType.MESH
LANES = 128
NZ, NY, NX = 8, 4, 4
PLANE = NY * NX
PAIRS = [(p, q) for p in range(4) for q in range(p, 4)]


def pair_of(p, q):
    return PAIRS.index((min(p, q), max(p, q)))


STEPS = [[(0, 0)], [(-1, 1), (1, -1)], [(-2, 1), (2, -1)], [(-3, 1), (3, -1)], [(4, 0)]]
RELS = [rel for step in STEPS for rel, _ in step]


def kernel(
    row_s, col_s, own_s, x_hbm, occ, virt, out,
    xb, vb, zb, ab, hot, part, tiles, red_z, plane_tile, red_p,
    xsem, p1s, p1r, zs, zr, cs, cr, fs, fr, ss, sr, rs, rr, ps, pr,
):
    blk, core = lax.axis_index("blk"), lax.axis_index("aux")
    z, y, x = blk // PLANE, (blk // NX) % NY, blk % NX
    other = 1 - core
    blocks, groups = row_s.shape[0], occ.shape[0]
    bs = occ.shape[1]
    mine = blocks // 2
    rows = x_hbm.shape[0] // 2

    def chip(zi, yi, xi):
        return (zi * NY + yi) * NX + xi

    def at(zi, yi, xi, ci):
        return {"blk": chip(zi, yi, xi), "aux": ci}

    def up(v, d, n):
        return (v + d) % n

    own_copy = pltpu.make_async_copy(x_hbm.at[pl.ds(core * rows, rows)], xb.at[core], xsem.at[0])
    own_copy.start()
    for i in range(2):
        low = virt[2 * core + i]
        high = virt[2 * core + i + groups // 2]
        vb[z, y, x, 2 * core + i] = jnp.concatenate([low, high], axis=1)

    greet = (
        [at(z, up(y, d, NY), x, core) for d in range(1, NY)]
        + [at(z, y, up(x, d, NX), core) for d in range(1, NX)]
        + [at(up(z, d, NZ), y, x, core) for d in (1, NZ - 1)]
        + [at(z, y, x, other)]
    )
    barrier = pltpu.get_barrier_semaphore()
    for device in greet:
        pl.semaphore_signal(barrier, inc=1, device_id=device, device_id_type=MESH)
    pl.semaphore_wait(barrier, len(greet))

    started = []

    def send(src, dst, ssem, rsem, device):
        copy = pltpu.make_async_remote_copy(
            src_ref=src, dst_ref=dst, send_sem=ssem, recv_sem=rsem, device_id=device, device_id_type=MESH
        )
        copy.start()
        started.append(copy)

    def arrived(region, ssem, rsem):
        pltpu.make_async_remote_copy(
            src_ref=region, dst_ref=region, send_sem=ssem, recv_sem=rsem,
            device_id=at(z, y, x, other), device_id_type=MESH,
        ).wait_recv()

    first = (y, x)
    last = (x, y)

    def region(p, zi, lo, count, ci, owner=None):
        tile = 2 * (core if owner is None else owner) + p
        if p == 0:
            return vb.at[zi, pl.ds(lo, count), ci, tile]
        return vb.at[zi, ci, pl.ds(lo, count), tile]

    def peer(p, zi, ai, ci):
        return at(zi, ai, ci, core) if p == 0 else at(zi, ci, ai, core)

    for p in range(2):
        for d in (1, 3, 2):
            src = region(p, z, first[p], 1, last[p])
            send(src, src, p1s.at[p, d], p1r.at[p, d], peer(p, z, up(first[p], d, 4), last[p]))
    send(
        x_hbm.at[pl.ds(other * rows, rows)], xb.at[core], xsem.at[1], xsem.at[2], at(z, y, x, other)
    )

    source = lax.broadcasted_iota(jnp.int32, (bs, bs), 0)
    column = lax.broadcasted_iota(jnp.int32, (bs, bs), 1)
    picks = [
        ((source == 2 * (column // 2) + lo) & (column % 2 == p)).astype(jnp.bfloat16)
        for lo in range(2)
        for p in range(2)
    ]

    def left_factor(g, carry):
        block = occ[g]
        for i, pick in enumerate(picks):
            piece = lax.dot_general(block, pick, (((0,), (0,)), ((), ())), preferred_element_type=jnp.float32)
            ab[g, i * bs:(i + 1) * bs, :] = piece.astype(jnp.bfloat16)
        return carry

    lax.fori_loop(0, groups, left_factor, 0)
    own_copy.wait()

    lane = lax.broadcasted_iota(jnp.int32, (bs, LANES), 1)
    low_half = lane < bs
    group_lane = lax.broadcasted_iota(jnp.int32, (1, hot.shape[1]), 1)
    base = core * mine

    def half_blocks(start, count):
        def one(k, carry):
            a = ab[row_s[base + k]]
            at_row = pl.multiple_of(k * bs, bs)
            both = jnp.concatenate([xb[0, pl.ds(at_row, bs), :], xb[1, pl.ds(at_row, bs), :]], axis=1)
            wide = jnp.dot(a, both, preferred_element_type=jnp.float32)
            for cc in range(2):
                t = [wide[i * bs:(i + 1) * bs, cc * LANES:(cc + 1) * LANES] for i in range(4)]
                straight = jnp.where(low_half, t[0], t[3])
                crossed = jnp.where(low_half, t[1], t[2])
                half = straight + pltpu.roll(crossed, bs, 1)
                zb[k, cc * bs:(cc + 1) * bs, :] = half.astype(jnp.bfloat16)
            group = own_s[base + k] * groups + col_s[base + k]
            hot[pl.ds(k, 1), :] = (group_lane == group).astype(jnp.float32)
            return carry

        lax.fori_loop(start, start + count, one, 0)

    def forward_last(step):
        for p in range(2):
            for rel, _ in STEPS[step]:
                j = RELS.index(rel)
                zi = up(z, rel, NZ)
                for s, d in enumerate((1, 3)):
                    ci = up(last[p], -d, 4)
                    arrived(region(p, zi, 0, 4, ci), cs.at[p, s, j], cr.at[p, s, j])
                    piece = region(p, zi, 2 * s, 2, ci)
                    send(piece, piece, fs.at[p, s, j], fr.at[p, s, j], peer(p, zi * 0 + z, first[p], up(last[p], d, 4)))

    def pass_on(step):
        for p in range(2):
            for rel, _ in STEPS[step]:
                j = RELS.index(rel)
                zi = up(z, rel, NZ)
                for s in range(2):
                    piece = region(p, zi, 2 * s, 2, up(last[p], 2, 4))
                    arrived(piece, fs.at[p, s, j], fr.at[p, s, j])
                whole = vb.at[zi, :, :, 2 * core + p]
                send(whole, whole, ss.at[p, j], sr.at[p, j], at(z, y, x, other))

    exchanged = False
    done = 0
    for step, members in enumerate(STEPS):
        for p in range(2):
            if step == 0:
                for d in range(1, 4):
                    got = region(p, z, up(first[p], -d, 4), 1, last[p])
                    arrived(got, p1s.at[p, d], p1r.at[p, d])
            for rel, way in members:
                zi = up(z, rel, NZ)
                if step == 4:
                    for s in range(2):
                        arrived(region(p, zi, 2 * s, 2, last[p]), zs.at[p, s, 3], zr.at[p, s, 3])
                    continue
                for s, d in enumerate((1, -1)):
                    if way not in (0, d):
                        continue
                    if step:
                        arrived(region(p, zi, 0, 4, last[p]), zs.at[p, s, step - 1], zr.at[p, s, step - 1])
                    piece = region(p, zi, 0, 4, last[p]) if step < 3 else region(p, zi, 2 * s, 2, last[p])
                    send(piece, piece, zs.at[p, s, step], zr.at[p, s, step], peer(p, up(z, d, NZ), first[p], last[p]))
        for p in range(2):
            for rel, _ in members:
                j = RELS.index(rel)
                piece = region(p, up(z, rel, NZ), 0, 4, last[p])
                for s, d in enumerate((1, 3)):
                    send(piece, piece, cs.at[p, s, j], cr.at[p, s, j], peer(p, z, first[p], up(last[p], d, 4)))
        if not exchanged:
            got = xb.at[other]
            arrived(got, xsem.at[1], xsem.at[2])
            exchanged = True
        count = mine // 8
        half_blocks(done, count)
        done += count
        if step >= 1:
            forward_last(step - 1)
        if step >= 2:
            pass_on(step - 2)
    half_blocks(done, mine - done)
    forward_last(4)
    pass_on(3)
    pass_on(4)

    for p in range(2):
        for rel in RELS:
            j = RELS.index(rel)
            arrived(vb.at[up(z, rel, NZ), :, :, 2 * other + p], ss.at[p, j], sr.at[p, j])

    zero = jnp.zeros((bs, LANES), jnp.bfloat16)
    lane_half = lax.broadcasted_iota(jnp.int32, (8, LANES), 1) // bs

    def full_block(k, carry):
        owner, slot = own_s[base + k], col_s[base + k]
        tile = vb[owner // PLANE, (owner // NX) % NY, owner % NX, slot % (groups // 2)]
        right = jnp.concatenate(
            [jnp.concatenate([tile, zero], axis=1), jnp.concatenate([zero, tile], axis=1)], axis=0
        )
        full = jnp.dot(zb[k], right, preferred_element_type=jnp.float32)
        full = full.astype(jnp.bfloat16).astype(jnp.float32)
        f = [full[cc * bs:(cc + 1) * bs, p * LANES:(p + 1) * LANES] for cc in range(2) for p in range(2)]
        keep = lane_half == slot // (groups // 2)
        at_row = pl.multiple_of(k * 8, 8)
        for i, (p, q) in enumerate(PAIRS):
            folded = jnp.sum((f[p] * f[q]).reshape(bs // 8, 8, LANES), axis=0)
            part[pl.ds(i * mine * 8 + at_row, 8), :] = jnp.where(keep, folded, 0.0)
        return carry

    lax.fori_loop(0, mine, full_block, 0)

    def thirds(value):
        one = value.astype(jnp.bfloat16)
        rest = value - one.astype(jnp.float32)
        two = rest.astype(jnp.bfloat16)
        return one, two, (rest - two.astype(jnp.float32)).astype(jnp.bfloat16)

    count = len(PAIRS) * mine
    lines = part[pl.ds(0, count, stride=8), :]
    for i in range(1, 8):
        lines = lines + part[pl.ds(i, count, stride=8), :]
    ones = jnp.ones((16, LANES), jnp.bfloat16)
    sums = sum(
        lax.dot_general(ones, t, (((1,), (1,)), ((), ())), preferred_element_type=jnp.float32)
        for t in thirds(lines)
    )
    out_row = lax.broadcasted_iota(jnp.int32, (16, LANES), 0)
    out_half = lax.broadcasted_iota(jnp.int32, (16, LANES), 1) // bs
    left = jnp.zeros((16, LANES), jnp.float32)
    for i in range(len(PAIRS)):
        chosen = functools.reduce(
            jnp.logical_or, [out_row == 4 * p + q for p in range(4) for q in range(4) if pair_of(p, q) == i]
        )
        column = sums[:, (i // 2) * LANES:(i // 2 + 1) * LANES]
        left = left + jnp.where(chosen & (out_half == i % 2), column, 0.0)
    left = left * (0.25 / (bs * bs))
    onehot = hot[...].astype(jnp.bfloat16)
    onehot = jnp.concatenate([onehot, onehot], axis=0)
    chi = jnp.dot(jnp.concatenate(thirds(left), axis=0), onehot, preferred_element_type=jnp.float32)
    chi = chi[0:16] + chi[16:32] + chi[32:48]
    for cc in range(2):
        for zi in range(NZ):
            tiles[cc, zi] = chi[cc * 8:(cc + 1) * 8, zi * LANES:(zi + 1) * LANES]

    for d in range(NZ):
        for cc in range(2):
            target = (core + cc) % 2
            if d == 0 and cc == 0:
                continue
            zi = up(z, d, NZ)
            send(tiles.at[target, zi], red_z.at[d, cc], rs.at[d, cc], rr.at[d, cc], at(zi, y, x, target))
    total = tiles[core, z]
    for d in range(NZ):
        for cc in range(2):
            if d == 0 and cc == 0:
                continue
            arrived(red_z.at[d, cc], rs.at[d, cc], rr.at[d, cc])
            total = total + red_z[d, cc]
    plane_tile[...] = total
    for dy in range(NY):
        for dx in range(NX):
            if dy == 0 and dx == 0:
                continue
            send(plane_tile, red_p.at[dy, dx], ps.at[dy, dx], pr.at[dy, dx], at(z, up(y, dy, NY), up(x, dx, NX), core))
    for dy in range(NY):
        for dx in range(NX):
            if dy == 0 and dx == 0:
                continue
            arrived(red_p.at[dy, dx], ps.at[dy, dx], pr.at[dy, dx])
            total = total + red_p[dy, dx]
    start = (y * NX + x) * groups
    total = pltpu.roll(total, (LANES - start) % LANES, 1)
    out[0] = total[0:4, 0:groups]
    out[1] = total[4:8, 0:groups]
    for copy in started:
        copy.wait_send()


def body(three_centre, occupied_blocks, virtual_blocks, row_slot, col_slot, block_owner):
    blocks, aux_local, width = three_centre.shape
    groups, bs, _ = occupied_blocks.shape
    mine = blocks // 2
    lines = three_centre.reshape(blocks, aux_local, width // LANES, LANES)
    lines = lines.transpose(0, 2, 1, 3).reshape(-1, LANES)
    dma = pltpu.SemaphoreType.DMA
    result = pl.pallas_call(
        kernel,
        out_shape=jax.ShapeDtypeStruct((2, 4, groups), jnp.float32),
        in_specs=[pl.BlockSpec(memory_space=pltpu.SMEM)] * 3
        + [pl.BlockSpec(memory_space=pl.ANY)]
        + [pl.BlockSpec(memory_space=pltpu.VMEM)] * 2,
        out_specs=pl.BlockSpec(memory_space=pltpu.VMEM),
        scratch_shapes=[
            pltpu.VMEM((2, lines.shape[0] // 2, LANES), jnp.bfloat16),
            pltpu.VMEM((NZ, NY, NX, groups // 2, bs, LANES), jnp.bfloat16),
            pltpu.VMEM((mine, 2 * bs, LANES), jnp.bfloat16),
            pltpu.VMEM((groups, 4 * bs, bs), jnp.bfloat16),
            pltpu.VMEM((mine, NZ * NY * NX * groups), jnp.float32),
            pltpu.VMEM((len(PAIRS) * mine * 8, LANES), jnp.float32),
            pltpu.VMEM((2, NZ, 8, LANES), jnp.float32),
            pltpu.VMEM((NZ, 2, 8, LANES), jnp.float32),
            pltpu.VMEM((8, LANES), jnp.float32),
            pltpu.VMEM((NY, NX, 8, LANES), jnp.float32),
            dma((3,)),
            dma((2, 4)), dma((2, 4)),
            dma((2, 2, 4)), dma((2, 2, 4)),
            dma((2, 2, 8)), dma((2, 2, 8)),
            dma((2, 2, 8)), dma((2, 2, 8)),
            dma((2, 8)), dma((2, 8)),
            dma((NZ, 2)), dma((NZ, 2)),
            dma((NY, NX)), dma((NY, NX)),
        ],
        compiler_params=pltpu.CompilerParams(
            collective_id=0, has_side_effects=True
        ),
    )(row_slot, col_slot, block_owner[:, 0], lines, occupied_blocks, virtual_blocks)
    return result.transpose(2, 0, 1)


def solution(mesh):
    in_specs = (
        P("blk", "aux", None),
        P("blk", None, None),
        P("blk", None, None),
        P("blk"),
        P("blk"),
        P("blk", None),
    )
    return jax.shard_map(body, mesh=mesh, in_specs=in_specs, out_specs=P("blk", "aux", None), check_vma=False)
```

```python
import functools

import jax
import jax.numpy as jnp
from jax import lax
from jax.experimental import pallas as pl
from jax.experimental.pallas import tpu as pltpu
from jax.sharding import PartitionSpec as P

MESH = pl.DeviceIdType.MESH
LANES = 128
NZ, NY, NX = 8, 4, 4
UNROLL_HALF, UNROLL_FULL = 4, 8
PLANE = NY * NX
PAIRS = [(p, q) for p in range(4) for q in range(p, 4)]


def pair_of(p, q):
    return PAIRS.index((min(p, q), max(p, q)))


STEPS = [[(0, 0)], [(-1, 1), (1, -1)], [(-2, 1), (2, -1)], [(-3, 1), (3, -1)], [(4, 0)]]
RELS = [rel for step in STEPS for rel, _ in step]


def kernel(
    row_s, col_s, own_s, x_hbm, occ, virt, out,
    xb, vb, zb, ab, hot, part, tiles, red_z, plane_tile, red_p,
    xsem, p1r, zr, cr, fr, sems,
):
    blk, core = lax.axis_index("blk"), lax.axis_index("aux")
    z, y, x = blk // PLANE, (blk // NX) % NY, blk % NX
    other = 1 - core
    blocks, groups = row_s.shape[0], occ.shape[0]
    bs = occ.shape[1]
    mine = blocks // 2
    rows = x_hbm.shape[0] // 2

    def chip(zi, yi, xi):
        return (zi * NY + yi) * NX + xi

    def at(zi, yi, xi, ci):
        return {"blk": chip(zi, yi, xi), "aux": ci}

    def up(v, d, n):
        return (v + d) % n

    own_copy = pltpu.make_async_copy(x_hbm.at[pl.ds(core * rows, rows)], xb.at[core], xsem.at[0])
    own_copy.start()
    for i in range(2):
        low = virt[2 * core + i]
        high = virt[2 * core + i + groups // 2]
        vb[z, y, x, 2 * core + i] = jnp.concatenate([low, high], axis=1)

    greet = (
        [at(z, up(y, d, NY), x, core) for d in range(1, NY)]
        + [at(z, y, up(x, d, NX), core) for d in range(1, NX)]
        + [at(up(z, d, NZ), y, x, core) for d in (1, NZ - 1)]
        + [at(z, y, x, other)]
    )
    barrier = pltpu.get_barrier_semaphore()
    for device in greet:
        pl.semaphore_signal(barrier, inc=1, device_id=device, device_id_type=MESH)
    pl.semaphore_wait(barrier, len(greet))

    p1s, zs, cs, fs, ss, sr, rs, rr, ps, pr = [sems.at[i] for i in range(10)]

    def send(src, dst, ssem, rsem, device):
        copy = pltpu.make_async_remote_copy(
            src_ref=src, dst_ref=dst, send_sem=ssem, recv_sem=rsem, device_id=device, device_id_type=MESH
        )
        copy.start()

    def transfer(region, sem):
        return pltpu.make_async_remote_copy(
            src_ref=region, dst_ref=region, send_sem=sem, recv_sem=sem,
            device_id=at(z, y, x, other), device_id_type=MESH,
        )

    def arrived(region, sem):
        transfer(region, sem).wait_recv()

    def left(region, sem):
        transfer(region, sem).wait_send()

    first = (y, x)
    last = (x, y)

    def region(p, zi, lo, count, ci, owner=None):
        tile = 2 * (core if owner is None else owner) + p
        if p == 0:
            return vb.at[zi, pl.ds(lo, count), ci, tile]
        return vb.at[zi, ci, pl.ds(lo, count), tile]

    def peer(p, zi, ai, ci):
        return at(zi, ai, ci, core) if p == 0 else at(zi, ci, ai, core)

    for p in range(2):
        for d in (1, 3, 2):
            src = region(p, z, first[p], 1, last[p])
            send(src, src, p1s, p1r.at[p], peer(p, z, up(first[p], d, 4), last[p]))
    send(
        x_hbm.at[pl.ds(other * rows, rows)], xb.at[core], xsem.at[1], xsem.at[2], at(z, y, x, other)
    )

    source = lax.broadcasted_iota(jnp.int32, (bs, bs), 0)
    column = lax.broadcasted_iota(jnp.int32, (bs, bs), 1)
    picks = [
        ((source == 2 * (column // 2) + lo) & (column % 2 == p)).astype(jnp.bfloat16)
        for lo in range(2)
        for p in range(2)
    ]

    def left_factor(g, carry):
        block = occ[g]
        for i, pick in enumerate(picks):
            piece = lax.dot_general(block, pick, (((0,), (0,)), ((), ())), preferred_element_type=jnp.float32)
            ab[g, i * bs:(i + 1) * bs, :] = piece.astype(jnp.bfloat16)
        return carry

    lax.fori_loop(0, groups, left_factor, 0)

    lane = lax.broadcasted_iota(jnp.int32, (bs, LANES), 1)
    low_half = lane < bs
    group_lane = lax.broadcasted_iota(jnp.int32, (1, hot.shape[1]), 1)
    base = core * mine

    def half_blocks(start, count):
        def one(k):
            a = ab[row_s[base + k]]
            at_row = pl.multiple_of(k * bs, bs)
            both = jnp.concatenate([xb[0, pl.ds(at_row, bs), :], xb[1, pl.ds(at_row, bs), :]], axis=1)
            wide = jnp.dot(a, both, preferred_element_type=jnp.float32)
            half = []
            for cc in range(2):
                t = [wide[i * bs:(i + 1) * bs, cc * LANES:(cc + 1) * LANES] for i in range(4)]
                straight = jnp.where(low_half, t[0], t[3])
                crossed = jnp.where(low_half, t[1], t[2])
                half.append(straight + pltpu.roll(crossed, bs, 1))
            mixed = [half[cc][i:i + 8] for i in range(0, bs, 8) for cc in range(2)]
            zb[k] = jnp.concatenate(mixed, axis=0).astype(jnp.bfloat16)
            group = own_s[base + k] * groups + col_s[base + k]
            hot[pl.ds(k, 1), :] = (group_lane == group).astype(jnp.float32)

        def some(i, carry):
            for k in range(UNROLL_HALF):
                one(start + i * UNROLL_HALF + k)
            return carry

        lax.fori_loop(0, count // UNROLL_HALF, some, 0)

    def forward_last(step):
        for p in range(2):
            for rel, _ in STEPS[step]:
                j = RELS.index(rel)
                zi = up(z, rel, NZ)
                for s, d in enumerate((1, 3)):
                    ci = up(last[p], -d, 4)
                    arrived(region(p, zi, 0, 4, ci), cr.at[p, s, j])
                    piece = region(p, zi, 2 * s, 2, ci)
                    send(piece, piece, fs, fr.at[p, j], peer(p, z, first[p], up(last[p], d, 4)))

    def pass_on(step):
        for p in range(2):
            for rel, _ in STEPS[step]:
                j = RELS.index(rel)
                zi = up(z, rel, NZ)
                arrived(region(p, zi, 0, 4, up(last[p], 2, 4)), fr.at[p, j])
                whole = vb.at[zi, :, :, 2 * core + p]
                send(whole, whole, ss, sr, at(z, y, x, other))

    exchanged = False
    done = 0
    for step, members in enumerate(STEPS):
        for p in range(2):
            if step == 0:
                arrived(region(p, z, 0, 3, last[p]), p1r.at[p])
            for rel, way in members:
                zi = up(z, rel, NZ)
                if step == 4:
                    for s in range(2):
                        arrived(region(p, zi, 2 * s, 2, last[p]), zr.at[p, s, 3])
                    continue
                for s, d in enumerate((1, -1)):
                    if way not in (0, d):
                        continue
                    if step:
                        arrived(region(p, zi, 0, 4, last[p]), zr.at[p, s, step - 1])
                    piece = region(p, zi, 0, 4, last[p]) if step < 3 else region(p, zi, 2 * s, 2, last[p])
                    send(piece, piece, zs, zr.at[p, s, step], peer(p, up(z, d, NZ), first[p], last[p]))
        for p in range(2):
            for rel, _ in members:
                j = RELS.index(rel)
                piece = region(p, up(z, rel, NZ), 0, 4, last[p])
                for s, d in enumerate((1, 3)):
                    send(piece, piece, cs, cr.at[p, s, j], peer(p, z, first[p], up(last[p], d, 4)))
        if not exchanged:
            got = xb.at[other]
            arrived(got, xsem.at[2])
            own_copy.wait()
            exchanged = True
        count = mine // 8
        half_blocks(done, count)
        done += count
        if step >= 1:
            forward_last(step - 1)
        if step >= 2:
            pass_on(step - 2)
    half_blocks(done, mine - done)
    forward_last(4)
    pass_on(3)
    pass_on(4)

    arrived(vb.at[:, :, :, pl.ds(2 * other, 2)], sr)

    zero = jnp.zeros((bs, LANES), jnp.bfloat16)
    lane_half = lax.broadcasted_iota(jnp.int32, (8, LANES), 1) // bs

    def full_block(k):
        owner, slot = own_s[base + k], col_s[base + k]
        tile = vb[owner // PLANE, (owner // NX) % NY, owner % NX, slot % (groups // 2)]
        right = jnp.concatenate(
            [jnp.concatenate([tile, zero], axis=1), jnp.concatenate([zero, tile], axis=1)], axis=0
        )
        full = jnp.dot(zb[k], right, preferred_element_type=jnp.float32)
        full = full.astype(jnp.bfloat16).astype(jnp.float32)
        keep = lane_half == slot // (groups // 2)
        at_row = pl.multiple_of(k * 8, 8)
        folded = [None] * len(PAIRS)
        for i in range(0, 2 * bs, 16):
            f = [
                full[i + 8 * cc:i + 8 * cc + 8, p * LANES:(p + 1) * LANES] for cc in range(2) for p in range(2)
            ]
            for n, (p, q) in enumerate(PAIRS):
                term = f[p] * f[q]
                folded[n] = term if folded[n] is None else folded[n] + term
        for n in range(len(PAIRS)):
            part[pl.ds(n * mine * 8 + at_row, 8), :] = jnp.where(keep, folded[n], 0.0)

    def some_full(i, carry):
        for k in range(UNROLL_FULL):
            full_block(i * UNROLL_FULL + k)
        return carry

    lax.fori_loop(0, mine // UNROLL_FULL, some_full, 0)

    def thirds(value):
        one = value.astype(jnp.bfloat16)
        rest = value - one.astype(jnp.float32)
        two = rest.astype(jnp.bfloat16)
        return one, two, (rest - two.astype(jnp.float32)).astype(jnp.bfloat16)

    count = len(PAIRS) * mine
    lines = part[pl.ds(0, count, stride=8), :]
    for i in range(1, 8):
        lines = lines + part[pl.ds(i, count, stride=8), :]
    ones = jnp.ones((16, LANES), jnp.bfloat16)
    sums = sum(
        lax.dot_general(ones, t, (((1,), (1,)), ((), ())), preferred_element_type=jnp.float32)
        for t in thirds(lines)
    )
    out_row = lax.broadcasted_iota(jnp.int32, (16, LANES), 0)
    out_half = lax.broadcasted_iota(jnp.int32, (16, LANES), 1) // bs
    lhs = jnp.zeros((16, LANES), jnp.float32)
    for i in range(len(PAIRS)):
        chosen = functools.reduce(
            jnp.logical_or, [out_row == 4 * p + q for p in range(4) for q in range(4) if pair_of(p, q) == i]
        )
        column = sums[:, (i // 2) * LANES:(i // 2 + 1) * LANES]
        lhs = lhs + jnp.where(chosen & (out_half == i % 2), column, 0.0)
    lhs = lhs * (0.25 / (bs * bs))
    onehot = hot[...].astype(jnp.bfloat16)
    onehot = jnp.concatenate([onehot, onehot], axis=0)
    chi = jnp.dot(jnp.concatenate(thirds(lhs), axis=0), onehot, preferred_element_type=jnp.float32)
    chi = chi[0:16] + chi[16:32] + chi[32:48]
    for cc in range(2):
        for zi in range(NZ):
            tiles[cc, zi] = chi[cc * 8:(cc + 1) * 8, zi * LANES:(zi + 1) * LANES]

    for d in range(NZ):
        for cc in range(2):
            target = (core + cc) % 2
            if d == 0 and cc == 0:
                continue
            zi = up(z, d, NZ)
            send(tiles.at[target, zi], red_z.at[2 * d + cc], rs, rr, at(zi, y, x, target))
    arrived(red_z.at[pl.ds(1, 2 * NZ - 1)], rr)
    total = tiles[core, z] + jnp.sum(red_z[1:], axis=0)
    plane_tile[...] = total
    for dy in range(NY):
        for dx in range(NX):
            if dy == 0 and dx == 0:
                continue
            send(plane_tile, red_p.at[dy * NX + dx], ps, pr, at(z, up(y, dy, NY), up(x, dx, NX), core))
    arrived(red_p.at[pl.ds(1, PLANE - 1)], pr)
    total = total + jnp.sum(red_p[1:], axis=0)
    start = (y * NX + x) * groups
    total = pltpu.roll(total, (LANES - start) % LANES, 1)
    out[0] = total[0:4, 0:groups]
    out[1] = total[4:8, 0:groups]
    left(x_hbm.at[pl.ds(0, rows)], xsem.at[1])
    left(vb.at[0, pl.ds(0, 3), 0, pl.ds(0, 2)], p1s)
    left(vb.at[pl.ds(0, 7), :, pl.ds(0, 2), 0], zs)
    left(vb.at[:, :, :, 0], cs)
    left(vb.at[:, :, pl.ds(0, 2), 0], fs)
    left(vb.at[:, :, :, pl.ds(0, 2)], ss)
    left(red_z.at[pl.ds(1, 2 * NZ - 1)], rs)
    left(red_p.at[pl.ds(1, PLANE - 1)], ps)


def body(three_centre, occupied_blocks, virtual_blocks, row_slot, col_slot, block_owner):
    blocks, aux_local, width = three_centre.shape
    groups, bs, _ = occupied_blocks.shape
    mine = blocks // 2
    lines = three_centre.reshape(blocks, aux_local, width // LANES, LANES)
    lines = lines.transpose(0, 2, 1, 3).reshape(-1, LANES)
    dma = pltpu.SemaphoreType.DMA
    result = pl.pallas_call(
        kernel,
        out_shape=jax.ShapeDtypeStruct((2, 4, groups), jnp.float32),
        in_specs=[pl.BlockSpec(memory_space=pltpu.SMEM)] * 3
        + [pl.BlockSpec(memory_space=pl.ANY)]
        + [pl.BlockSpec(memory_space=pltpu.VMEM)] * 2,
        out_specs=pl.BlockSpec(memory_space=pltpu.VMEM),
        scratch_shapes=[
            pltpu.VMEM((2, lines.shape[0] // 2, LANES), jnp.bfloat16),
            pltpu.VMEM((NZ, NY, NX, groups // 2, bs, LANES), jnp.bfloat16),
            pltpu.VMEM((mine, 2 * bs, LANES), jnp.bfloat16),
            pltpu.VMEM((groups, 4 * bs, bs), jnp.bfloat16),
            pltpu.VMEM((mine, NZ * NY * NX * groups), jnp.float32),
            pltpu.VMEM((len(PAIRS) * mine * 8, LANES), jnp.float32),
            pltpu.VMEM((2, NZ, 8, LANES), jnp.float32),
            pltpu.VMEM((2 * NZ, 8, LANES), jnp.float32),
            pltpu.VMEM((8, LANES), jnp.float32),
            pltpu.VMEM((PLANE, 8, LANES), jnp.float32),
            dma((3,)), dma((2,)), dma((2, 2, 4)), dma((2, 2, 8)), dma((2, 8)), dma((10,)),
        ],
        compiler_params=pltpu.CompilerParams(
            collective_id=0, has_side_effects=True
        ),
    )(row_slot, col_slot, block_owner[:, 0], lines, occupied_blocks, virtual_blocks)
    return result.transpose(2, 0, 1)


def solution(mesh):
    in_specs = (
        P("blk", "aux", None),
        P("blk", None, None),
        P("blk", None, None),
        P("blk"),
        P("blk"),
        P("blk", None),
    )
    return jax.shard_map(body, mesh=mesh, in_specs=in_specs, out_specs=P("blk", "aux", None), check_vma=False)
```
